32 devices in a mesh: leaf: 4 (over y, x), col: 8 (over z, core).
Axes of the slice: x: 2, y: 2, z: 4, core: 2. Of those that a mesh axis runs over, the one named last changes fastest.
Arguments:
- s_blocks: bfloat16 [64, 8, 128, 128], P(('leaf', 'col')), may hold values from -0.0059814453 to 0.0059814453
- z_blocks: bfloat16 [64, 8, 128, 128], P(('leaf', 'col')), may hold values from -1.5 to 1.5
- s_requests: int32 [4, 8, 8, 1], P('leaf', 'col'), may hold values from -1 to 15, as said below
- y_pairs: int32 [64, 8, 8], P(('leaf', 'col')), may hold values from -1 to 7, as said below
- zt_requests: int32 [4, 8, 8, 1], P('leaf', 'col'), may hold values from -1 to 31, as said below
- d_pairs: int32 [64, 8, 8], P(('leaf', 'col')), may hold values from -1 to 7, as said below
- d_requests: int32 [4, 8, 8, 1], P('leaf', 'col'), may hold values from -1 to 31, as said below
- e_pairs: int32 [64, 8, 8], P(('leaf', 'col')), may hold values from -1 to 7, as said below
- z_requests: int32 [4, 8, 8, 1], P('leaf', 'col'), may hold values from -1 to 31, as said below
- z_pairs: int32 [64, 8, 8], P(('leaf', 'col')), may hold values from -1 to 7, as said below
Outputs:
- z_refined: bfloat16 [64, 8, 128, 128], P(('leaf', 'col'))
The draws below stay inside these ranges and needn't reach their ends.
Inputs may be any that keep to these rules, and one draw needn't show every extreme that they name: `s_requests`: entry [l, c, p, q] is -1 or a slot of the S holdings of the device (l, p); the entries of one [l, c, p] are distinct. Every reader has some peer with all 1 entries used, and one reader uses all entries. `zt_requests`: entry [l, c, p, q] is -1 or a slot of the Z holdings of the device (l, p); the entries of one [l, c, p] are distinct. Every reader has some peer with all 1 entries used, and one reader uses all entries. `d_requests`: entry [l, c, p, q] is -1 or a slot of the D holdings of the device (l, p); the entries of one [l, c, p] are distinct. Every reader has some peer with all 1 entries used, and one reader uses all entries. `z_requests`: entry [l, c, p, q] is -1 or a slot of the Z holdings of the device (l, p); the entries of one [l, c, p] are distinct. Every reader has some peer with all 1 entries used, and one reader uses all entries. `y_pairs`: each entry is -1 or the position p + q of an entry of s_requests that is not -1, for the reader holding the column; every such entry is named at least once. `d_pairs`: each entry is -1 or the position p + q of an entry of zt_requests that is not -1, for the reader holding the column; every such entry is named at least once. `e_pairs`: each entry is -1 or the position p + q of an entry of d_requests that is not -1, for the reader holding the column; every such entry is named at least once. `z_pairs`: each entry is -1 or the position p + q of an entry of z_requests that is not -1, for the reader holding the column; every such entry is named at least once.
All inputs are finite; a program needn't handle non-finite values.
Results may differ from the reference program's by a relative error of at most 0.0059.
Values may be sent and summed in bfloat16 or wider, within the bound.
A program may use at most 64 MiB of HBM per device.

```python
import jax
import jax.numpy as jnp
from jax import lax

BLOCK = 128
SLOTS = 8
CAP = 1
CD = 2
NBC = 64
N_LEAF = 4
N_COL = 8


def request_lists(key, hold_count):
    readers = N_LEAF * N_COL
    fetch_total = N_COL * CAP
    triples = CD * SLOTS * SLOTS
    subkeys = jax.random.split(key, 7)
    reader_load = jax.random.randint(subkeys[0], (readers, 1), 1, 4)
    counts = jnp.minimum(jax.random.randint(subkeys[1], (readers, N_COL), 0, 12) % (reader_load + 1), CAP)
    busy_peer = jax.random.randint(subkeys[2], (readers, 1), 0, N_COL)
    full_reader = jax.random.randint(subkeys[3], (), 0, readers)
    peer_ids = jnp.arange(N_COL)[None, :]
    reader_ids = jnp.arange(readers)[:, None]
    counts = jnp.where((peer_ids == busy_peer) | (reader_ids == full_reader), CAP, counts)
    scores = jax.random.randint(subkeys[4], (readers, N_COL, hold_count), 0, 1 << 20) * hold_count + jnp.arange(hold_count)
    ranked = jnp.argsort(scores, axis=-1)[:, :, :CAP]
    asked_ids = jnp.where(jnp.arange(CAP)[None, None, :] < counts[:, :, None], ranked, -1).astype(jnp.int32)
    live_mask = (asked_ids >= 0).reshape(readers, fetch_total)
    slot_scores = jax.random.randint(subkeys[5], (readers, triples), 0, 1 << 20) * triples + jnp.arange(triples)
    slot_order = jnp.argsort(slot_scores, axis=-1)
    position = jnp.broadcast_to(jnp.arange(triples)[None, :], (readers, triples))
    spare_ids = jax.random.randint(subkeys[6], (readers, triples), 0, fetch_total)
    wanted = jnp.where(position < fetch_total, position, spare_ids)
    wanted_live = jnp.take_along_axis(live_mask, wanted, axis=-1)
    entries = jnp.where(wanted_live, wanted, -1)
    inverse = jnp.argsort(slot_order, axis=-1)
    pair_ids = jnp.take_along_axis(entries, inverse, axis=-1).astype(jnp.int32)
    return (asked_ids.reshape(N_LEAF, N_COL, N_COL, CAP), pair_ids.reshape(NBC, SLOTS, SLOTS))


def draw_s_requests(key, part):
    return request_lists(jax.random.fold_in(key, 11), CD * SLOTS)[0]


def draw_y_pairs(key, part):
    return request_lists(jax.random.fold_in(key, 11), CD * SLOTS)[1]


def draw_zt_requests(key, part):
    return request_lists(jax.random.fold_in(key, 12), 2 * CD * SLOTS)[0]


def draw_d_pairs(key, part):
    return request_lists(jax.random.fold_in(key, 12), 2 * CD * SLOTS)[1]


def draw_d_requests(key, part):
    return request_lists(jax.random.fold_in(key, 13), 2 * CD * SLOTS)[0]


def draw_e_pairs(key, part):
    return request_lists(jax.random.fold_in(key, 13), 2 * CD * SLOTS)[1]


def draw_z_requests(key, part):
    return request_lists(jax.random.fold_in(key, 14), 2 * CD * SLOTS)[0]


def draw_z_pairs(key, part):
    return request_lists(jax.random.fold_in(key, 14), 2 * CD * SLOTS)[1]


def block_levels(stream_key, dims, cuts, smallest, high):
    def one(dim, parts):
        draws = jax.random.uniform(jax.random.fold_in(jax.random.fold_in(stream_key, 6), dim), (parts,), jnp.float32, smallest / len(cuts), high / len(cuts))
        return jnp.repeat(jnp.exp(draws), dims[dim] // parts).reshape((-1,) + (1,) * (len(dims) - dim - 1))

    gain = one(*cuts[0])
    for cut in cuts[1:]:
        gain = gain * one(*cut)
    return gain


def gaussian(stream_key, extent, spread, bound, shards=(), kind=jnp.bfloat16):
    array = spread * jax.random.normal(stream_key, extent, jnp.float32)
    if shards:
        array = array * block_levels(stream_key, extent, shards, -0.22, 0.18)
    return jnp.clip(array, -bound, bound).astype(kind)


def setup_inputs(seed: int = 0) -> dict:
    key_list = jax.random.split(jax.random.key(seed), 11)
    return {
        "s_blocks": gaussian(key_list[0], (NBC, SLOTS, BLOCK, BLOCK), 0.001, 0.0059814453, ((0, 32),)),
        "z_blocks": gaussian(key_list[1], (NBC, SLOTS, BLOCK, BLOCK), 0.25, 1.5, ((0, 32),)),
        "s_requests": draw_s_requests(jax.random.fold_in(key_list[10], 71), 0),
        "y_pairs": draw_y_pairs(jax.random.fold_in(key_list[10], 71), 0),
        "zt_requests": draw_zt_requests(jax.random.fold_in(key_list[10], 71), 0),
        "d_pairs": draw_d_pairs(jax.random.fold_in(key_list[10], 71), 0),
        "d_requests": draw_d_requests(jax.random.fold_in(key_list[10], 71), 0),
        "e_pairs": draw_e_pairs(jax.random.fold_in(key_list[10], 71), 0),
        "z_requests": draw_z_requests(jax.random.fold_in(key_list[10], 71), 0),
        "z_pairs": draw_z_pairs(jax.random.fold_in(key_list[10], 71), 0),
    }


def holdings_of(blocks):
    return blocks.reshape(N_LEAF, N_COL, CD * SLOTS, BLOCK, BLOCK)


def fetch_for(own_blocks, requests, reader):
    hold_count = own_blocks.shape[2]
    leaf_index = reader // N_COL
    partner = leaf_index + 1 - 2 * (leaf_index % 2)
    from_partner = requests >= hold_count
    source_leaf = jnp.where(from_partner, partner, leaf_index).astype(jnp.int32)
    source_slot = jnp.maximum(jnp.where(from_partner, requests - hold_count, requests), 0).astype(jnp.int32)
    peer_ids = jnp.broadcast_to(jnp.arange(N_COL, dtype=jnp.int32)[:, None], requests.shape)
    blocks = own_blocks[source_leaf, peer_ids, source_slot]
    blocks = jnp.where((requests >= 0)[:, :, None, None], blocks, jnp.zeros_like(blocks))
    return blocks.reshape(N_COL * CAP, BLOCK, BLOCK)


def block_products(fetched, pair_ids, local_blocks, flipped):
    fetch_count = fetched.shape[0]
    padded = jnp.concatenate([fetched, jnp.zeros((1,) + fetched.shape[1:], fetched.dtype)], axis=0)
    lookup = jnp.where(pair_ids < 0, fetch_count, pair_ids).astype(jnp.int32)
    chosen = jnp.take(padded, lookup, axis=0).astype(jnp.float32)
    einsum_form = "gabji,gbjk->gaik" if flipped else "gabij,gbjk->gaik"
    return jnp.einsum(einsum_form, chosen, local_blocks.astype(jnp.float32))


def product_pass(own_blocks, requests, pair_ids, local_blocks, flipped):
    readers = N_LEAF * N_COL
    asked_ids = requests.reshape(readers, N_COL, CAP)
    paired = pair_ids.reshape(readers, CD, SLOTS, SLOTS)
    local_rows = local_blocks.reshape(readers, CD, SLOTS, BLOCK, BLOCK)

    def one_reader(packed):
        reader, reader_asks, reader_pairs, reader_local = packed
        fetched = fetch_for(own_blocks, reader_asks, reader)
        return block_products(fetched, reader_pairs, reader_local, flipped)

    result = lax.map(one_reader, (jnp.arange(readers, dtype=jnp.int32), asked_ids, paired, local_rows))
    return result.reshape(NBC, SLOTS, BLOCK, BLOCK)


def reference(s_blocks, z_blocks, s_requests, y_pairs, zt_requests, d_pairs, d_requests, e_pairs, z_requests, z_pairs):
    s_own = holdings_of(s_blocks)
    z_own = holdings_of(z_blocks)
    y_blocks = product_pass(s_own, s_requests, y_pairs, z_blocks, False).astype(jnp.bfloat16)
    first_slot = (jnp.arange(SLOTS) == 0).astype(jnp.float32)
    identity = first_slot[:, None, None] * jnp.eye(BLOCK, dtype=jnp.float32)
    d_blocks = (identity - product_pass(z_own, zt_requests, d_pairs, y_blocks, True)).astype(jnp.bfloat16)
    square = product_pass(holdings_of(d_blocks), d_requests, e_pairs, d_blocks, False)
    e_blocks = (0.5 * d_blocks.astype(jnp.float32) + 0.375 * square).astype(jnp.bfloat16)
    refined = z_blocks.astype(jnp.float32) + product_pass(z_own, z_requests, z_pairs, e_blocks, False)
    return refined.astype(jnp.bfloat16)
```

```python
import functools

import jax
import jax.numpy as jnp
from jax import lax
from jax.experimental import pallas as pl
from jax.experimental.pallas import tpu as pltpu
from jax.sharding import PartitionSpec as P

MESH = pl.DeviceIdType.MESH
S, T, Z, D = range(4)


def kernel(
    n,
    cap,
    cols,
    slots,
    req_ref,
    pairs_ref,
    s_ref,
    z_ref,
    out_ref,
    allreq,
    send_s,
    send_t,
    send_z,
    send_d,
    xs_t,
    xs_z,
    xs_d,
    xr_t,
    xr_z,
    xr_d,
    f_s,
    f_t,
    f_z,
    f_d,
    y_ref,
    d_ref,
    e_ref,
    req_send,
    req_recv,
    own_sem,
    z_send,
    z_recv,
    x_send,
    x_recv,
):
    leaf = lax.axis_index("leaf")
    me = lax.axis_index("col")
    partner = leaf + 1 - 2 * lax.rem(leaf, 2)
    hold = cols * slots
    size = z_ref.shape[1]
    fetch = n * cap
    sends = {S: send_s, T: send_t, Z: send_z, D: send_d}
    fetched = {S: f_s, T: f_t, Z: f_z, D: f_d}
    xsends = {T: xs_t, Z: xs_z, D: xs_d}
    xrecvs = {T: xr_t, Z: xr_z, D: xr_d}

    def loop(count, body):
        def step(k, carry):
            body(k)
            return carry

        lax.fori_loop(0, count, step, 0)

    def at(k):
        return lax.rem(me + k, n)

    barrier = pltpu.get_barrier_semaphore()

    def greet_own(k):
        pl.semaphore_signal(barrier, inc=1, device_id=(leaf, at(k + 1)), device_id_type=MESH)

    def greet_other(k):
        pl.semaphore_signal(barrier, inc=1, device_id=(partner, at(k)), device_id_type=MESH)

    loop(n - 1, greet_own)
    loop(n, greet_other)
    for f in (f_s, f_t, f_z, f_d):
        f[fetch] = jnp.zeros((size, size), f.dtype)
    own_copy = pltpu.make_async_copy(req_ref, allreq.at[me], own_sem)
    own_copy.start()
    pl.semaphore_wait(barrier, 2 * n - 1)

    def req_copy(side, to_leaf, to, source):
        return pltpu.make_async_remote_copy(
            src_ref=req_ref,
            dst_ref=allreq.at[side * n + source],
            send_sem=req_send.at[side * n + to],
            recv_sem=req_recv.at[side * n + source],
            device_id=(to_leaf, to),
            device_id_type=MESH,
        )

    loop(n - 1, lambda k: req_copy(0, leaf, at(k + 1), me).start())
    loop(n, lambda k: req_copy(1, partner, at(k), me).start())
    own_copy.wait()
    loop(n - 1, lambda k: req_copy(0, leaf, at(k + 1), at(k + 1)).wait_recv())
    loop(n, lambda k: req_copy(1, partner, at(k), at(k)).wait_recv())

    def ask(kind, side, c, q):
        word = kind * fetch + me * cap + q
        return allreq[side * n + c, lax.div(word, 128), lax.rem(word, 128)]

    def x_copy(kind, c):
        span = pl.ds(c * cap, cap)
        return pltpu.make_async_remote_copy(
            src_ref=xsends[kind].at[span],
            dst_ref=xrecvs[kind].at[span],
            send_sem=x_send.at[kind, c],
            recv_sem=x_recv.at[kind, c],
            device_id=(partner, me),
            device_id_type=MESH,
        )

    def z_copy(kind, to, source):
        return pltpu.make_async_remote_copy(
            src_ref=sends[kind].at[pl.ds(to * cap, cap)],
            dst_ref=fetched[kind].at[pl.ds(source * cap, cap)],
            send_sem=z_send.at[kind, to],
            recv_sem=z_recv.at[kind, source],
            device_id=(leaf, to),
            device_id_type=MESH,
        )

    def x_pass(kind, own_ref):
        def body(k):
            c = at(k)
            for q in range(cap):
                slot = jnp.clip(ask(kind, 1, c, q) - hold, 0, hold - 1)
                xsends[kind][c * cap + q] = own_ref[slot]
            x_copy(kind, c).start()

        return body

    def chosen(kind, own_ref, c, q):
        request = ask(kind, 0, c, q)
        block = own_ref[jnp.clip(request, 0, hold - 1)]
        if kind != S:
            block = jnp.where(request < hold, block, xrecvs[kind][c * cap + q])
        if kind == T:
            block = block.T
        return block

    def z_pass(kind, own_ref):
        def body(k):
            c = at(k + 1)
            if kind != S:
                x_copy(kind, c).wait_recv()
            for q in range(cap):
                sends[kind][c * cap + q] = chosen(kind, own_ref, c, q)
            z_copy(kind, c, me).start()

        loop(n - 1, body)
        if kind != S:
            x_copy(kind, me).wait_recv()
        for q in range(cap):
            fetched[kind][me * cap + q] = chosen(kind, own_ref, me, q)

    def arrived(kind):
        loop(n - 1, lambda k: z_copy(kind, at(k + 1), at(k + 1)).wait_recv())

    def x_order(k):
        return lax.rem(k + 1, n)

    def product(kind, base, local_ref, finish):
        f = fetched[kind]

        def body(a):
            for g in range(cols):
                row = base * cols * slots * slots + (g * slots + a) * slots
                blocks = []
                for b in range(slots):
                    name = pairs_ref[row + b]
                    blocks.append(f[jnp.where(name < 0, fetch, name)])
                lhs = jnp.concatenate(blocks, axis=1)
                rhs = local_ref[pl.ds(g * slots, slots)].reshape(slots * size, size)
                finish(g * slots + a, a, jnp.dot(lhs, rhs, preferred_element_type=jnp.float32))

        loop(slots, body)

    def x_start(kind, own_ref):
        body = x_pass(kind, own_ref)
        loop(n, lambda k: body(x_order(k)))

    z_pass(S, s_ref)
    x_start(T, z_ref)
    x_start(Z, z_ref)
    z_pass(T, z_ref)

    arrived(S)

    def y_finish(i, a, total):
        y_ref[i] = total.astype(y_ref.dtype)

    product(S, 0, z_ref, y_finish)
    z_pass(Z, z_ref)
    arrived(T)

    def d_finish(i, a, total):
        rows = lax.broadcasted_iota(jnp.int32, (size, size), 0)
        columns = lax.broadcasted_iota(jnp.int32, (size, size), 1)
        first = jnp.where(a == 0, 1.0, 0.0)
        d_ref[i] = (jnp.where(rows == columns, first, 0.0) - total).astype(d_ref.dtype)

    product(T, 1, y_ref, d_finish)
    x_start(D, d_ref)
    z_pass(D, d_ref)
    arrived(D)

    def e_finish(i, a, total):
        e_ref[i] = (0.5 * d_ref[i].astype(jnp.float32) + 0.375 * total).astype(e_ref.dtype)

    product(D, 2, d_ref, e_finish)
    arrived(Z)

    def z_finish(i, a, total):
        out_ref[i] = (z_ref[i].astype(jnp.float32) + total).astype(out_ref.dtype)

    product(Z, 3, e_ref, z_finish)

    loop(n - 1, lambda k: req_copy(0, leaf, at(k + 1), me).wait_send())
    loop(n, lambda k: req_copy(1, partner, at(k), me).wait_send())
    for kind in (S, T, Z, D):
        loop(n - 1, lambda k: z_copy(kind, at(k + 1), me).wait_send())
        if kind != S:
            loop(n, lambda k: x_copy(kind, k).wait_send())


def on_device(
    n,
    s_blocks,
    z_blocks,
    s_requests,
    y_pairs,
    zt_requests,
    d_pairs,
    d_requests,
    e_pairs,
    z_requests,
    z_pairs,
):
    cols, slots, size = z_blocks.shape[:3]
    cap = s_requests.shape[3]
    hold = cols * slots
    flat = (hold, size, size)
    fetch = n * cap
    requests = jnp.concatenate(
        [r.reshape(-1) for r in (s_requests, zt_requests, z_requests, d_requests)]
    )
    rows = pl.cdiv(requests.shape[0], 128)
    requests = jnp.pad(requests, (0, rows * 128 - requests.shape[0])).reshape(rows, 128)
    pairs = jnp.concatenate([p.reshape(-1) for p in (y_pairs, d_pairs, e_pairs, z_pairs)])
    kind = z_blocks.dtype

    def blocks(count):
        return pltpu.VMEM((count, size, size), kind)

    vmem = pl.BlockSpec(memory_space=pltpu.VMEM)
    smem = pl.BlockSpec(memory_space=pltpu.SMEM)
    refined = pl.pallas_call(
        functools.partial(kernel, n, cap, cols, slots),
        out_shape=jax.ShapeDtypeStruct(flat, kind),
        in_specs=[vmem, smem, vmem, vmem],
        out_specs=vmem,
        scratch_shapes=[pltpu.SMEM((2 * n, rows, 128), jnp.int32)]
        + [blocks(fetch) for _ in range(10)]
        + [blocks(fetch + 1) for _ in range(4)]
        + [blocks(hold) for _ in range(3)]
        + [
            pltpu.SemaphoreType.DMA((2 * n,)),
            pltpu.SemaphoreType.DMA((2 * n,)),
            pltpu.SemaphoreType.DMA,
            pltpu.SemaphoreType.DMA((4, n)),
            pltpu.SemaphoreType.DMA((4, n)),
            pltpu.SemaphoreType.DMA((4, n)),
            pltpu.SemaphoreType.DMA((4, n)),
        ],
        compiler_params=pltpu.CompilerParams(
            collective_id=0, has_side_effects=True, vmem_limit_bytes=48 * 1024 * 1024
        ),
    )(requests, pairs, s_blocks.reshape(flat), z_blocks.reshape(flat))
    return refined.reshape(z_blocks.shape)


def solution(mesh):
    flat4 = P(("leaf", "col"), None, None, None)
    flat3 = P(("leaf", "col"), None, None)
    asks = P("leaf", "col", None, None)
    in_specs = (flat4, flat4, asks, flat3, asks, flat3, asks, flat3, asks, flat3)
    return jax.shard_map(
        functools.partial(on_device, mesh.shape["col"]),
        mesh=mesh,
        in_specs=in_specs,
        out_specs=flat4,
        check_vma=False,
    )
```

```python
import functools

import jax
import jax.numpy as jnp
from jax import lax
from jax.experimental import pallas as pl
from jax.experimental.pallas import tpu as pltpu
from jax.sharding import PartitionSpec as P

MESH = pl.DeviceIdType.MESH
S, T, Z, D = range(4)


def kernel(
    n,
    cap,
    cols,
    slots,
    s_asks,
    t_asks,
    z_asks,
    d_asks,
    y_names,
    d_names,
    e_names,
    z_names,
    s_hbm,
    z_hbm,
    out_hbm,
    req_ref,
    allreq,
    y_pairs,
    d_pairs,
    e_pairs,
    z_pairs,
    s_ref,
    z_ref,
    out_ref,
    send_s,
    send_t,
    send_z,
    send_d,
    xs_t,
    xs_z,
    xs_d,
    xr_t,
    xr_z,
    xr_d,
    f_s,
    f_t,
    f_z,
    f_d,
    y_ref,
    d_ref,
    e_ref,
    req_send,
    req_recv,
    own_sem,
    in_sem,
    out_sem,
    z_send,
    z_recv,
    x_send,
    x_recv,
):
    leaf = lax.axis_index("leaf")
    me = lax.axis_index("col")
    partner = leaf + 1 - 2 * lax.rem(leaf, 2)
    hold = cols * slots
    size = z_ref.shape[1]
    fetch = n * cap
    pairs = {S: y_pairs, T: d_pairs, D: e_pairs, Z: z_pairs}
    asks = (s_asks, t_asks, z_asks, d_asks)
    moves = [(a, req_ref.at[pl.ds(kind, 1)]) for kind, a in enumerate(asks)]
    moves += [(s_hbm, s_ref), (z_hbm, z_ref)]
    moves += [(y_names, y_pairs), (d_names, d_pairs), (e_names, e_pairs), (z_names, z_pairs)]
    loads = [pltpu.make_async_copy(a, b, in_sem.at[i]) for i, (a, b) in enumerate(moves)]
    sends = {S: send_s, T: send_t, Z: send_z, D: send_d}
    fetched = {S: f_s, T: f_t, Z: f_z, D: f_d}
    xsends = {T: xs_t, Z: xs_z, D: xs_d}
    xrecvs = {T: xr_t, Z: xr_z, D: xr_d}

    def loop(count, body):
        def step(k, carry):
            body(k)
            return carry

        lax.fori_loop(0, count, step, 0)

    def at(k):
        if n & (n - 1):
            return lax.rem(me + k, n)
        mask = lax.rem(jnp.int32(n) - k, n)
        total, bit = 0, 1
        while bit < n:
            total += lax.rem(lax.div(me, bit) + lax.div(mask, bit), 2) * bit
            bit *= 2
        return total

    barrier = pltpu.get_barrier_semaphore()

    def greet_own(k):
        pl.semaphore_signal(barrier, inc=1, device_id=(leaf, at(k + 1)), device_id_type=MESH)

    def greet_other(k):
        pl.semaphore_signal(barrier, inc=1, device_id=(partner, at(k)), device_id_type=MESH)

    loop(n - 1, greet_own)
    loop(n, greet_other)
    for load in loads:
        load.start()
    for f in (f_s, f_t, f_z, f_d):
        f[fetch] = jnp.zeros((size, size), f.dtype)
    own_copy = pltpu.make_async_copy(req_ref, allreq.at[me], own_sem)
    for load in loads[:4]:
        load.wait()
    own_copy.start()
    pl.semaphore_wait(barrier, 2 * n - 1)

    def req_copy(side, to_leaf, to, source):
        return pltpu.make_async_remote_copy(
            src_ref=req_ref,
            dst_ref=allreq.at[side * n + source],
            send_sem=req_send.at[side * n + to],
            recv_sem=req_recv.at[side * n + source],
            device_id=(to_leaf, to),
            device_id_type=MESH,
        )

    loop(n - 1, lambda k: req_copy(0, leaf, at(k + 1), me).start())
    loop(n, lambda k: req_copy(1, partner, at(k), me).start())
    own_copy.wait()
    for load in loads[4:]:
        load.wait()

    def ask(kind, side, c, q):
        return allreq[side * n + c, kind, me * cap + q]

    def x_copy(kind, c):
        span = pl.ds(c * cap, cap)
        return pltpu.make_async_remote_copy(
            src_ref=xsends[kind].at[span],
            dst_ref=xrecvs[kind].at[span],
            send_sem=x_send.at[kind, c],
            recv_sem=x_recv.at[kind, c],
            device_id=(partner, me),
            device_id_type=MESH,
        )

    def z_copy(kind, to, source):
        return pltpu.make_async_remote_copy(
            src_ref=sends[kind].at[pl.ds(to * cap, cap)],
            dst_ref=fetched[kind].at[pl.ds(source * cap, cap)],
            send_sem=z_send.at[kind, to],
            recv_sem=z_recv.at[kind, source],
            device_id=(leaf, to),
            device_id_type=MESH,
        )

    def x_pass(kind, own_ref):
        def body(k):
            c = at(k)
            if kind == T:
                req_copy(1, partner, c, c).wait_recv()
            for q in range(cap):
                slot = jnp.clip(ask(kind, 1, c, q) - hold, 0, hold - 1)
                xsends[kind][c * cap + q] = own_ref[slot]
            x_copy(kind, c).start()

        return body

    def chosen(kind, own_ref, c, q):
        request = ask(kind, 0, c, q)
        block = own_ref[jnp.clip(request, 0, hold - 1)]
        if kind != S:
            block = jnp.where(request < hold, block, xrecvs[kind][c * cap + q])
        if kind == T:
            block = block.T
        return block

    def z_pass(kind, own_ref):
        def body(k):
            c = at(k + 1)
            if kind == S:
                req_copy(0, leaf, c, c).wait_recv()
            else:
                x_copy(kind, c).wait_recv()
            for q in range(cap):
                sends[kind][c * cap + q] = chosen(kind, own_ref, c, q)
            z_copy(kind, c, me).start()

        loop(n - 1, body)
        if kind != S:
            x_copy(kind, me).wait_recv()
        for q in range(cap):
            fetched[kind][me * cap + q] = chosen(kind, own_ref, me, q)

    def arrived(kind):
        loop(n - 1, lambda k: z_copy(kind, at(k + 1), at(k + 1)).wait_recv())

    def x_order(k):
        return lax.rem(k + 1, n)

    def product(kind, local_ref, finish, close=None):
        f = fetched[kind]

        def body(g):
            rhs = local_ref[pl.ds(g * slots, slots)].reshape(slots * size, size)
            for a in range(slots):
                blocks = []
                for b in range(slots):
                    name = pairs[kind][g, a, b]
                    blocks.append(f[jnp.where(name < 0, fetch, name)])
                lhs = jnp.concatenate(blocks, axis=1)
                finish(g * slots + a, a, jnp.dot(lhs, rhs, preferred_element_type=jnp.float32))
            if close is not None:
                close(g)

        lax.fori_loop(0, cols, lambda g, c: (body(g), c)[1], 0, unroll=True)

    def x_start(kind, own_ref):
        body = x_pass(kind, own_ref)
        loop(n, lambda k: body(x_order(k)))

    z_pass(S, s_ref)
    x_start(T, z_ref)
    x_start(Z, z_ref)
    z_pass(T, z_ref)

    arrived(S)

    def y_finish(i, a, total):
        y_ref[i] = total.astype(y_ref.dtype)

    product(S, z_ref, y_finish)
    z_pass(Z, z_ref)
    arrived(T)

    def d_finish(i, a, total):
        rows = lax.broadcasted_iota(jnp.int32, (size, size), 0)
        columns = lax.broadcasted_iota(jnp.int32, (size, size), 1)
        first = 1.0 if a == 0 else 0.0
        d_ref[i] = (jnp.where(rows == columns, first, 0.0) - total).astype(d_ref.dtype)

    product(T, y_ref, d_finish)
    x_start(D, d_ref)
    z_pass(D, d_ref)
    arrived(D)

    def e_finish(i, a, total):
        e_ref[i] = (0.5 * d_ref[i].astype(jnp.float32) + 0.375 * total).astype(e_ref.dtype)

    product(D, d_ref, e_finish)
    arrived(Z)

    def z_finish(i, a, total):
        out_ref[i] = (z_ref[i].astype(jnp.float32) + total).astype(out_ref.dtype)

    def out_copy(g):
        span = pl.ds(g * slots, slots)
        return pltpu.make_async_copy(out_ref.at[span], out_hbm.at[span], out_sem.at[g])

    product(Z, e_ref, z_finish, lambda g: out_copy(g).start())
    loop(cols, lambda g: out_copy(g).wait())

    loop(n - 1, lambda k: req_copy(0, leaf, at(k + 1), me).wait_send())
    loop(n, lambda k: req_copy(1, partner, at(k), me).wait_send())
    for kind in (S, T, Z, D):
        loop(n - 1, lambda k: z_copy(kind, at(k + 1), me).wait_send())
        if kind != S:
            loop(n, lambda k: x_copy(kind, k).wait_send())


def on_device(
    n,
    s_blocks,
    z_blocks,
    s_requests,
    y_pairs,
    zt_requests,
    d_pairs,
    d_requests,
    e_pairs,
    z_requests,
    z_pairs,
):
    cols, slots, size = z_blocks.shape[:3]
    cap = s_requests.shape[3]
    hold = cols * slots
    flat = (hold, size, size)
    fetch = n * cap
    asks = [
        r.reshape(1, fetch) for r in (s_requests, zt_requests, z_requests, d_requests)
    ]
    names = [y_pairs, d_pairs, e_pairs, z_pairs]
    kind = z_blocks.dtype

    def blocks(count):
        return pltpu.VMEM((count, size, size), kind)

    hbm = pl.BlockSpec(memory_space=pltpu.HBM)
    refined = pl.pallas_call(
        functools.partial(kernel, n, cap, cols, slots),
        out_shape=jax.ShapeDtypeStruct(flat, kind),
        in_specs=[hbm] * 10,
        out_specs=hbm,
        scratch_shapes=[
            pltpu.SMEM((4, fetch), jnp.int32),
            pltpu.SMEM((2 * n, 4, fetch), jnp.int32),
        ]
        + [pltpu.SMEM(y_pairs.shape, jnp.int32) for _ in range(4)]
        + [blocks(hold) for _ in range(3)]
        + [blocks(fetch) for _ in range(10)]
        + [blocks(fetch + 1) for _ in range(4)]
        + [blocks(hold) for _ in range(3)]
        + [
            pltpu.SemaphoreType.DMA((2 * n,)),
            pltpu.SemaphoreType.DMA((2 * n,)),
            pltpu.SemaphoreType.DMA,
            pltpu.SemaphoreType.DMA((10,)),
            pltpu.SemaphoreType.DMA((cols,)),
            pltpu.SemaphoreType.DMA((4, n)),
            pltpu.SemaphoreType.DMA((4, n)),
            pltpu.SemaphoreType.DMA((4, n)),
            pltpu.SemaphoreType.DMA((4, n)),
        ],
        compiler_params=pltpu.CompilerParams(
            collective_id=0, has_side_effects=True, vmem_limit_bytes=67043328
        ),
    )(*asks, *names, s_blocks.reshape(flat), z_blocks.reshape(flat))
    return refined.reshape(z_blocks.shape)


def solution(mesh):
    flat4 = P(("leaf", "col"), None, None, None)
    flat3 = P(("leaf", "col"), None, None)
    asks = P("leaf", "col", None, None)
    in_specs = (flat4, flat4, asks, flat3, asks, flat3, asks, flat3, asks, flat3)
    return jax.shard_map(
        functools.partial(on_device, mesh.shape["col"]),
        mesh=mesh,
        in_specs=in_specs,
        out_specs=flat4,
        check_vma=False,
    )
```

```python
import functools

import jax
import jax.numpy as jnp
from jax import lax
from jax.experimental import pallas as pl
from jax.experimental.pallas import tpu as pltpu
from jax.sharding import PartitionSpec as P

MESH = pl.DeviceIdType.MESH
S, T, Z, D = range(4)


def kernel(
    n,
    cap,
    cols,
    slots,
    s_asks,
    t_asks,
    z_asks,
    d_asks,
    y_names,
    d_names,
    e_names,
    z_names,
    s_hbm,
    z_hbm,
    out_ref,
    req_ref,
    allreq,
    y_pairs,
    d_pairs,
    e_pairs,
    z_pairs,
    s_ref,
    z_ref,
    send_s,
    send_t,
    send_z,
    send_d,
    xs_t,
    xs_z,
    xs_d,
    xr_t,
    xr_z,
    xr_d,
    f_s,
    f_t,
    f_z,
    f_d,
    y_ref,
    d_ref,
    e_ref,
    req_send,
    req_recv,
    own_sem,
    in_sem,
    z_send,
    z_recv,
    x_send,
    x_recv,
):
    leaf = lax.axis_index("leaf")
    me = lax.axis_index("col")
    partner = leaf + 1 - 2 * lax.rem(leaf, 2)
    hold = cols * slots
    size = z_ref.shape[1]
    fetch = n * cap
    pairs = {S: y_pairs, T: d_pairs, D: e_pairs, Z: z_pairs}
    asks = (s_asks, t_asks, z_asks, d_asks)
    moves = [(a, req_ref.at[pl.ds(kind, 1)]) for kind, a in enumerate(asks)]
    moves += [(s_hbm, s_ref), (z_hbm, z_ref)]
    moves += [(y_names, y_pairs), (d_names, d_pairs), (e_names, e_pairs), (z_names, z_pairs)]
    loads = [pltpu.make_async_copy(a, b, in_sem.at[i]) for i, (a, b) in enumerate(moves)]
    sends = {S: send_s, T: send_t, Z: send_z, D: send_d}
    fetched = {S: f_s, T: f_t, Z: f_z, D: f_d}
    xsends = {T: xs_t, Z: xs_z, D: xs_d}
    xrecvs = {T: xr_t, Z: xr_z, D: xr_d}

    def loop(count, body):
        def step(k, carry):
            body(k)
            return carry

        lax.fori_loop(0, count, step, 0)

    def at(k):
        if n & (n - 1):
            return lax.rem(me + k, n)
        mask = lax.rem(jnp.int32(n) - k, n)
        total, bit = 0, 1
        while bit < n:
            total += lax.rem(lax.div(me, bit) + lax.div(mask, bit), 2) * bit
            bit *= 2
        return total

    barrier = pltpu.get_barrier_semaphore()

    def greet_own(k):
        pl.semaphore_signal(barrier, inc=1, device_id=(leaf, at(k + 1)), device_id_type=MESH)

    def greet_other(k):
        pl.semaphore_signal(barrier, inc=1, device_id=(partner, at(k)), device_id_type=MESH)

    loop(n - 1, greet_own)
    loop(n, greet_other)
    for load in loads:
        load.start()
    for f in (f_s, f_t, f_z, f_d):
        f[fetch] = jnp.zeros((size, size), f.dtype)
    own_copy = pltpu.make_async_copy(req_ref, allreq.at[me], own_sem)
    for load in loads[:4]:
        load.wait()
    own_copy.start()
    pl.semaphore_wait(barrier, 2 * n - 1)

    def req_copy(side, to_leaf, to, source):
        return pltpu.make_async_remote_copy(
            src_ref=req_ref,
            dst_ref=allreq.at[side * n + source],
            send_sem=req_send.at[side * n + to],
            recv_sem=req_recv.at[side * n + source],
            device_id=(to_leaf, to),
            device_id_type=MESH,
        )

    loop(n - 1, lambda k: req_copy(0, leaf, at(k + 1), me).start())
    loop(n, lambda k: req_copy(1, partner, at(k), me).start())
    own_copy.wait()
    for load in loads[4:]:
        load.wait()

    def ask(kind, side, c, q):
        return allreq[side * n + c, kind, me * cap + q]

    def x_copy(kind, c):
        span = pl.ds(c * cap, cap)
        return pltpu.make_async_remote_copy(
            src_ref=xsends[kind].at[span],
            dst_ref=xrecvs[kind].at[span],
            send_sem=x_send.at[kind, c],
            recv_sem=x_recv.at[kind, c],
            device_id=(partner, me),
            device_id_type=MESH,
        )

    def z_copy(kind, to, source):
        return pltpu.make_async_remote_copy(
            src_ref=sends[kind].at[pl.ds(to * cap, cap)],
            dst_ref=fetched[kind].at[pl.ds(source * cap, cap)],
            send_sem=z_send.at[kind, to],
            recv_sem=z_recv.at[kind, source],
            device_id=(leaf, to),
            device_id_type=MESH,
        )

    def x_pass(kind, own_ref):
        def body(k):
            c = at(k)
            if kind == T:
                req_copy(1, partner, c, c).wait_recv()
            for q in range(cap):
                slot = jnp.clip(ask(kind, 1, c, q) - hold, 0, hold - 1)
                xsends[kind][c * cap + q] = own_ref[slot]
            x_copy(kind, c).start()

        return body

    def chosen(kind, own_ref, c, q):
        request = ask(kind, 0, c, q)
        block = own_ref[jnp.clip(request, 0, hold - 1)]
        if kind != S:
            block = jnp.where(request < hold, block, xrecvs[kind][c * cap + q])
        if kind == T:
            block = block.T
        return block

    def z_pass(kind, own_ref):
        def body(k):
            c = at(k + 1)
            if kind == S:
                req_copy(0, leaf, c, c).wait_recv()
            else:
                x_copy(kind, c).wait_recv()
            for q in range(cap):
                sends[kind][c * cap + q] = chosen(kind, own_ref, c, q)
            z_copy(kind, c, me).start()

        loop(n - 1, body)
        if kind != S:
            x_copy(kind, me).wait_recv()
        for q in range(cap):
            fetched[kind][me * cap + q] = chosen(kind, own_ref, me, q)

    def arrived(kind):
        loop(n - 1, lambda k: z_copy(kind, at(k + 1), at(k + 1)).wait_recv())

    def x_order(k):
        return lax.rem(k + 1, n)

    def product(kind, local_ref, finish, close=None):
        f = fetched[kind]

        def body(g):
            rhs = local_ref[pl.ds(g * slots, slots)].reshape(slots * size, size)
            for a in range(slots):
                blocks = []
                for b in range(slots):
                    name = pairs[kind][g, a, b]
                    blocks.append(f[jnp.where(name < 0, fetch, name)])
                lhs = jnp.concatenate(blocks, axis=1)
                finish(g * slots + a, a, jnp.dot(lhs, rhs, preferred_element_type=jnp.float32))
            if close is not None:
                close(g)

        lax.fori_loop(0, cols, lambda g, c: (body(g), c)[1], 0, unroll=True)

    def x_start(kind, own_ref):
        body = x_pass(kind, own_ref)
        loop(n, lambda k: body(x_order(k)))

    z_pass(S, s_ref)
    x_start(T, z_ref)
    x_start(Z, z_ref)
    z_pass(T, z_ref)

    arrived(S)

    def y_finish(i, a, total):
        y_ref[i] = total.astype(y_ref.dtype)

    product(S, z_ref, y_finish)
    z_pass(Z, z_ref)
    arrived(T)

    def d_finish(i, a, total):
        rows = lax.broadcasted_iota(jnp.int32, (size, size), 0)
        columns = lax.broadcasted_iota(jnp.int32, (size, size), 1)
        first = 1.0 if a == 0 else 0.0
        d_ref[i] = (jnp.where(rows == columns, first, 0.0) - total).astype(d_ref.dtype)

    product(T, y_ref, d_finish)
    x_start(D, d_ref)
    z_pass(D, d_ref)
    arrived(D)

    def e_finish(i, a, total):
        e_ref[i] = (0.5 * d_ref[i].astype(jnp.float32) + 0.375 * total).astype(e_ref.dtype)

    product(D, d_ref, e_finish)
    arrived(Z)

    def z_finish(i, a, total):
        out_ref[i] = (z_ref[i].astype(jnp.float32) + total).astype(out_ref.dtype)

    product(Z, e_ref, z_finish)

    loop(n - 1, lambda k: req_copy(0, leaf, at(k + 1), me).wait_send())
    loop(n, lambda k: req_copy(1, partner, at(k), me).wait_send())
    for kind in (S, T, Z, D):
        loop(n - 1, lambda k: z_copy(kind, at(k + 1), me).wait_send())
        if kind != S:
            loop(n, lambda k: x_copy(kind, k).wait_send())


def on_device(
    n,
    s_blocks,
    z_blocks,
    s_requests,
    y_pairs,
    zt_requests,
    d_pairs,
    d_requests,
    e_pairs,
    z_requests,
    z_pairs,
):
    cols, slots, size = z_blocks.shape[:3]
    cap = s_requests.shape[3]
    hold = cols * slots
    flat = (hold, size, size)
    fetch = n * cap
    asks = [
        r.reshape(1, fetch) for r in (s_requests, zt_requests, z_requests, d_requests)
    ]
    names = [y_pairs, d_pairs, e_pairs, z_pairs]
    kind = z_blocks.dtype

    def blocks(count):
        return pltpu.VMEM((count, size, size), kind)

    hbm = pl.BlockSpec(memory_space=pltpu.HBM)
    refined = pl.pallas_call(
        functools.partial(kernel, n, cap, cols, slots),
        out_shape=pltpu.VMEM(flat, kind),
        in_specs=[hbm] * 10,
        out_specs=pl.BlockSpec(memory_space=pltpu.VMEM),
        scratch_shapes=[
            pltpu.SMEM((4, fetch), jnp.int32),
            pltpu.SMEM((2 * n, 4, fetch), jnp.int32),
        ]
        + [pltpu.SMEM(y_pairs.shape, jnp.int32) for _ in range(4)]
        + [blocks(hold) for _ in range(2)]
        + [blocks(fetch) for _ in range(10)]
        + [blocks(fetch + 1) for _ in range(4)]
        + [blocks(hold) for _ in range(3)]
        + [
            pltpu.SemaphoreType.DMA((2 * n,)),
            pltpu.SemaphoreType.DMA((2 * n,)),
            pltpu.SemaphoreType.DMA,
            pltpu.SemaphoreType.DMA((10,)),
            pltpu.SemaphoreType.DMA((4, n)),
            pltpu.SemaphoreType.DMA((4, n)),
            pltpu.SemaphoreType.DMA((4, n)),
            pltpu.SemaphoreType.DMA((4, n)),
        ],
        compiler_params=pltpu.CompilerParams(
            collective_id=0, has_side_effects=True, vmem_limit_bytes=66326528
        ),
    )(*asks, *names, s_blocks.reshape(flat), z_blocks.reshape(flat))
    return refined.reshape(z_blocks.shape)


def solution(mesh):
    flat4 = P(("leaf", "col"), None, None, None)
    flat3 = P(("leaf", "col"), None, None)
    asks = P("leaf", "col", None, None)
    in_specs = (flat4, flat4, asks, flat3, asks, flat3, asks, flat3, asks, flat3)
    return jax.shard_map(
        functools.partial(on_device, mesh.shape["col"]),
        mesh=mesh,
        in_specs=in_specs,
        out_specs=flat4,
        check_vma=False,
    )
```

```python
import functools

import jax
import jax.numpy as jnp
from jax import lax
from jax.experimental import pallas as pl
from jax.experimental.pallas import tpu as pltpu
from jax.sharding import PartitionSpec as P

MESH = pl.DeviceIdType.MESH
S, T, Z, D = range(4)


def kernel(
    n,
    cap,
    cols,
    slots,
    s_asks,
    t_asks,
    z_asks,
    d_asks,
    y_names,
    d_names,
    e_names,
    z_names,
    s_hbm,
    z_hbm,
    out_ref,
    req_ref,
    allreq,
    y_pairs,
    d_pairs,
    e_pairs,
    z_pairs,
    s_ref,
    z_ref,
    send_s,
    send_t,
    send_z,
    send_d,
    xs_t,
    xs_z,
    xs_d,
    xr_t,
    xr_z,
    xr_d,
    f_s,
    f_t,
    f_z,
    f_d,
    y_ref,
    d_ref,
    e_ref,
    req_send,
    req_recv,
    own_sem,
    in_sem,
    z_send,
    z_recv,
    x_send,
    x_recv,
):
    leaf = lax.axis_index("leaf")
    me = lax.axis_index("col")
    partner = leaf + 1 - 2 * lax.rem(leaf, 2)
    hold = cols * slots
    size = z_ref.shape[1]
    fetch = n * cap
    pairs = {S: y_pairs, T: d_pairs, D: e_pairs, Z: z_pairs}
    asks = (s_asks, t_asks, z_asks, d_asks)
    moves = [(a, req_ref.at[pl.ds(kind, 1)]) for kind, a in enumerate(asks)]
    moves += [(s_hbm, s_ref), (z_hbm, z_ref)]
    moves += [(y_names, y_pairs), (d_names, d_pairs), (e_names, e_pairs), (z_names, z_pairs)]
    loads = [pltpu.make_async_copy(a, b, in_sem.at[i]) for i, (a, b) in enumerate(moves)]
    sends = {S: send_s, T: send_t, Z: send_z, D: send_d}
    fetched = {S: f_s, T: f_t, Z: f_z, D: f_d}
    xsends = {T: xs_t, Z: xs_z, D: xs_d}
    xrecvs = {T: xr_t, Z: xr_z, D: xr_d}

    def loop(count, body):
        def step(k, carry):
            body(k)
            return carry

        lax.fori_loop(0, count, step, 0, unroll=n <= 8)

    def at(k):
        if n & (n - 1):
            return lax.rem(me + k, n)
        mask = lax.rem(jnp.int32(n) - k, n)
        total, bit = 0, 1
        while bit < n:
            total += lax.rem(lax.div(me, bit) + lax.div(mask, bit), 2) * bit
            bit *= 2
        return total

    barrier = pltpu.get_barrier_semaphore()

    def greet_own(k):
        pl.semaphore_signal(barrier, inc=1, device_id=(leaf, at(k + 1)), device_id_type=MESH)

    def greet_other(k):
        pl.semaphore_signal(barrier, inc=1, device_id=(partner, at(k)), device_id_type=MESH)

    loop(n - 1, greet_own)
    loop(n, greet_other)
    for load in loads:
        load.start()
    for f in (f_s, f_t, f_z, f_d):
        f[fetch] = jnp.zeros((size, size), f.dtype)
    own_copy = pltpu.make_async_copy(req_ref, allreq.at[me], own_sem)
    for load in loads[:4]:
        load.wait()
    own_copy.start()
    pl.semaphore_wait(barrier, 2 * n - 1)

    def req_copy(side, to_leaf, to, source):
        return pltpu.make_async_remote_copy(
            src_ref=req_ref,
            dst_ref=allreq.at[side * n + source],
            send_sem=req_send.at[side * n + to],
            recv_sem=req_recv.at[side * n + source],
            device_id=(to_leaf, to),
            device_id_type=MESH,
        )

    loop(n - 1, lambda k: req_copy(0, leaf, at(k + 1), me).start())
    loop(n, lambda k: req_copy(1, partner, at(k), me).start())
    own_copy.wait()
    for load in loads[4:6]:
        load.wait()

    def ask(kind, side, c, q):
        return allreq[side * n + c, kind, me * cap + q]

    def x_copy(kind, c):
        span = pl.ds(c * cap, cap)
        return pltpu.make_async_remote_copy(
            src_ref=xsends[kind].at[span],
            dst_ref=xrecvs[kind].at[span],
            send_sem=x_send.at[kind, c],
            recv_sem=x_recv.at[kind, c],
            device_id=(partner, me),
            device_id_type=MESH,
        )

    def z_copy(kind, to, source):
        return pltpu.make_async_remote_copy(
            src_ref=sends[kind].at[pl.ds(to * cap, cap)],
            dst_ref=fetched[kind].at[pl.ds(source * cap, cap)],
            send_sem=z_send.at[kind, to],
            recv_sem=z_recv.at[kind, source],
            device_id=(leaf, to),
            device_id_type=MESH,
        )

    def x_pass(kind, own_ref):
        def body(k):
            c = at(k)
            if kind == T:
                req_copy(1, partner, c, c).wait_recv()
            for q in range(cap):
                slot = jnp.clip(ask(kind, 1, c, q) - hold, 0, hold - 1)
                xsends[kind][c * cap + q] = own_ref[slot]
            x_copy(kind, c).start()

        return body

    def chosen(kind, own_ref, c, q):
        request = ask(kind, 0, c, q)
        block = own_ref[jnp.clip(request, 0, hold - 1)]
        if kind != S:
            block = jnp.where(request < hold, block, xrecvs[kind][c * cap + q])
        if kind == T:
            block = block.T
        return block

    def z_pass(kind, own_ref):
        def body(k):
            c = at(k + 1)
            if kind == S:
                req_copy(0, leaf, c, c).wait_recv()
            else:
                x_copy(kind, c).wait_recv()
            for q in range(cap):
                sends[kind][c * cap + q] = chosen(kind, own_ref, c, q)
            z_copy(kind, c, me).start()

        loop(n - 1, body)
        if kind != S:
            x_copy(kind, me).wait_recv()
        for q in range(cap):
            fetched[kind][me * cap + q] = chosen(kind, own_ref, me, q)

    def arrived(kind):
        loop(n - 1, lambda k: z_copy(kind, at(k + 1), at(k + 1)).wait_recv())

    def x_order(k):
        return lax.rem(k + 1, n)

    def product(kind, local_ref, finish, close=None):
        f = fetched[kind]

        def body(g):
            rhs = local_ref[pl.ds(g * slots, slots)].reshape(slots * size, size)
            for a in range(slots):
                blocks = []
                for b in range(slots):
                    name = pairs[kind][g, a, b]
                    blocks.append(f[jnp.where(name < 0, fetch, name)])
                lhs = jnp.concatenate(blocks, axis=1)
                finish(g * slots + a, a, jnp.dot(lhs, rhs, preferred_element_type=jnp.float32))
            if close is not None:
                close(g)

        lax.fori_loop(0, cols, lambda g, c: (body(g), c)[1], 0, unroll=True)

    def x_start(kind, own_ref):
        body = x_pass(kind, own_ref)
        loop(n, lambda k: body(x_order(k)))

    z_pass(S, s_ref)
    x_start(T, z_ref)
    x_start(Z, z_ref)
    z_pass(T, z_ref)

    for load in loads[6:]:
        load.wait()
    arrived(S)

    def y_finish(i, a, total):
        y_ref[i] = total.astype(y_ref.dtype)

    product(S, z_ref, y_finish)
    z_pass(Z, z_ref)
    arrived(T)

    def d_finish(i, a, total):
        rows = lax.broadcasted_iota(jnp.int32, (size, size), 0)
        columns = lax.broadcasted_iota(jnp.int32, (size, size), 1)
        first = 1.0 if a == 0 else 0.0
        d_ref[i] = (jnp.where(rows == columns, first, 0.0) - total).astype(d_ref.dtype)

    product(T, y_ref, d_finish)
    x_start(D, d_ref)
    z_pass(D, d_ref)
    arrived(D)

    def e_finish(i, a, total):
        e_ref[i] = (0.5 * d_ref[i].astype(jnp.float32) + 0.375 * total).astype(e_ref.dtype)

    product(D, d_ref, e_finish)
    arrived(Z)

    def z_finish(i, a, total):
        out_ref[i] = (z_ref[i].astype(jnp.float32) + total).astype(out_ref.dtype)

    product(Z, e_ref, z_finish)

    loop(n - 1, lambda k: req_copy(0, leaf, at(k + 1), me).wait_send())
    loop(n, lambda k: req_copy(1, partner, at(k), me).wait_send())
    for kind in (S, T, Z, D):
        loop(n - 1, lambda k: z_copy(kind, at(k + 1), me).wait_send())
        if kind != S:
            loop(n, lambda k: x_copy(kind, k).wait_send())


def on_device(
    n,
    s_blocks,
    z_blocks,
    s_requests,
    y_pairs,
    zt_requests,
    d_pairs,
    d_requests,
    e_pairs,
    z_requests,
    z_pairs,
):
    cols, slots, size = z_blocks.shape[:3]
    cap = s_requests.shape[3]
    hold = cols * slots
    flat = (hold, size, size)
    fetch = n * cap
    asks = [
        r.reshape(1, fetch) for r in (s_requests, zt_requests, z_requests, d_requests)
    ]
    names = [y_pairs, d_pairs, e_pairs, z_pairs]
    kind = z_blocks.dtype

    def blocks(count):
        return pltpu.VMEM((count, size, size), kind)

    hbm = pl.BlockSpec(memory_space=pltpu.HBM)
    refined = pl.pallas_call(
        functools.partial(kernel, n, cap, cols, slots),
        out_shape=pltpu.VMEM(flat, kind),
        in_specs=[hbm] * 10,
        out_specs=pl.BlockSpec(memory_space=pltpu.VMEM),
        scratch_shapes=[
            pltpu.SMEM((4, fetch), jnp.int32),
            pltpu.SMEM((2 * n, 4, fetch), jnp.int32),
        ]
        + [pltpu.SMEM(y_pairs.shape, jnp.int32) for _ in range(4)]
        + [blocks(hold) for _ in range(2)]
        + [blocks(fetch) for _ in range(10)]
        + [blocks(fetch + 1) for _ in range(4)]
        + [blocks(hold) for _ in range(3)]
        + [
            pltpu.SemaphoreType.DMA((2 * n,)),
            pltpu.SemaphoreType.DMA((2 * n,)),
            pltpu.SemaphoreType.DMA,
            pltpu.SemaphoreType.DMA((10,)),
            pltpu.SemaphoreType.DMA((4, n)),
            pltpu.SemaphoreType.DMA((4, n)),
            pltpu.SemaphoreType.DMA((4, n)),
            pltpu.SemaphoreType.DMA((4, n)),
        ],
        compiler_params=pltpu.CompilerParams(
            collective_id=0, has_side_effects=True, vmem_limit_bytes=66326528
        ),
    )(*asks, *names, s_blocks.reshape(flat), z_blocks.reshape(flat))
    return refined.reshape(z_blocks.shape)


def solution(mesh):
    flat4 = P(("leaf", "col"), None, None, None)
    flat3 = P(("leaf", "col"), None, None)
    asks = P("leaf", "col", None, None)
    in_specs = (flat4, flat4, asks, flat3, asks, flat3, asks, flat3, asks, flat3)
    return jax.shard_map(
        functools.partial(on_device, mesh.shape["col"]),
        mesh=mesh,
        in_specs=in_specs,
        out_specs=flat4,
        check_vma=False,
    )
```
